128 devices in a mesh: fsdp: 2 (over core), expert: 64 (over z, y, x).
Axes of the slice: x: 4, y: 4, z: 4, core: 2. Of those that a mesh axis runs over, the one named last changes fastest.
Arguments:
- tokens: bfloat16 [8192, 4096], P(('fsdp', 'expert')), may hold values from -6 to 6
- expert_ids: int32 [8192, 8], P(('fsdp', 'expert')), may hold values from 0 to 63, all different within a row; in each aligned block of 64 rows (0 to 63, 64 to 127, ...) at most 9 rows name the same one
- route_weight: float32 [8192, 8], P(('fsdp', 'expert')), may hold values from 0.1 to 1
- gate_weight: bfloat16 [64, 768, 4096], P('expert', 'fsdp'), may hold values from -0.09375 to 0.09375
- up_weight: bfloat16 [64, 768, 4096], P('expert', 'fsdp'), may hold values from -0.09375 to 0.09375
- down_weight: bfloat16 [64, 768, 4096], P('expert', None, 'fsdp'), may hold values from -0.21875 to 0.21875
Outputs:
- mixed: bfloat16 [8192, 4096], P(('fsdp', 'expert'))
The draws below stay inside these ranges and needn't reach their ends.
Inputs may be any that keep to these rules, and one draw needn't show every extreme that they name: `expert_ids`: each row names 8 different experts; within the rows of one device no expert is named by more than 9 rows, a bound that some block reaches.
All inputs are finite; a program needn't handle non-finite values.
Results may differ from the reference program's by a relative error of at most 0.011.
Values may be sent and summed in bfloat16 or wider, within the bound.
No kernel may reach another device: no remote copies, remote signals or barrier semaphores. Data moves between devices by JAX's collectives and lax.ppermute only.
A program may use at most 128 MiB of HBM per device.

```python
import math
import jax
import jax.numpy as jnp
import numpy as np
from jax import lax

D = 4096
FF = 768
TOP = 8
TOK_DEV = 64
EXPERTS = 64
CAP = 9
TOKENS = 8192
N_FSDP = 2
N_EXPERT = 64


def steps_of(key, extent, pieces, smallest, high):
    loudness, own = 1.0, jax.random.fold_in(key, 6)
    for axis_at, parts in pieces:
        steps = jnp.exp(jax.random.uniform(jax.random.fold_in(own, axis_at), (parts,), jnp.float32, smallest / len(pieces), high / len(pieces)))
        loudness = loudness * jnp.repeat(steps, extent[axis_at] // parts).reshape([-1 if axis == axis_at else 1 for axis in range(len(extent))])
    return loudness


def routed_block(key, own, number, rows, amount, top, reach, skew):
    order = jax.random.permutation(key, amount)
    heavy_load, common = load_shares(amount, rows * top, reach, skew, True), load_shares(amount, rows * top, reach, skew, False)
    places = jnp.arange(amount)

    def named(lengths, offset_by):
        used = int((lengths > 0).sum())
        fixed = max(1, used // 4)
        passed = fixed + (places - fixed + offset_by * (used - fixed)) % max(1, amount - fixed)
        return jnp.zeros((amount,), jnp.int32).at[order[jnp.where(places < fixed, places, passed)]].set(jnp.asarray(lengths, jnp.int32))

    lengths = jnp.where(number % 4 == 0, named(heavy_load, number // 4), named(common, number - number // 4 - 1))
    mixed = jax.random.permutation(jax.random.fold_in(own, 3), amount)
    donor, sink = mixed[0:amount // 2 * 2:2], mixed[1:amount // 2 * 2:2]
    room = jnp.minimum(lengths[donor] - 1, reach - lengths[sink]) // 2
    room = jnp.where((donor == order[0]) | (sink == order[0]) | (lengths[sink] == 0), 0, jnp.maximum(room, 0))
    passed = jax.random.randint(jax.random.fold_in(own, 4), (amount // 2,), 0, 1 << 20) % (room + 1)
    lengths = lengths.at[donor].add(-passed).at[sink].add(passed)
    members = jnp.searchsorted(jnp.cumsum(lengths), jnp.arange(rows * top), side="right").astype(jnp.int32)
    grid = members.reshape(top, rows).T
    grid = grid[jax.random.permutation(jax.random.fold_in(own, 1), rows)]
    offset_by = jax.random.randint(jax.random.fold_in(own, 2), (rows, 1), 0, top)
    return jnp.take_along_axis(grid, (jnp.arange(top)[None, :] + offset_by) % top, axis=1)


def load_shares(amount, total, most, lean, full):
    loads = [(1 << 20) // math.isqrt(standing ** lean) + 1 for standing in range(1, amount + 1)]
    largest = most if full else min(most, max(-(-total // amount), total * loads[0] // sum(loads)))
    least = 1 if total - largest >= amount - 1 else 0
    holding, surplus = [largest] + [least] * (amount - 1), total - largest - least * (amount - 1)
    while surplus > 0:
        free = [i for i in range(1, amount) if holding[i] < largest] or [i for i in range(1, amount) if holding[i] < most]
        pool, remaining = sum([loads[i] for i in free]), surplus
        for i in free:
            more = min(most - holding[i], max(1, remaining * loads[i] // pool), surplus)
            holding[i] = holding[i] + more
            surplus = surplus - more
    return np.array(holding)


def noise(key, extent, deviation, reach, split=(), kind=jnp.bfloat16):
    result = deviation * jax.random.normal(key, extent, jnp.float32)
    if split:
        result = result * steps_of(key, extent, split, -0.22, 0.18)
    return jnp.clip(result, -reach, reach).astype(kind)


def setup_inputs(seed: int = 0) -> dict:
    arg_keys = jax.random.split(jax.random.key(seed), 7)
    tokens = noise(arg_keys[0], (TOKENS, D), 1.0, 6.0, ((0, 128),))
    expert_ids_keys = jax.random.split(jax.random.fold_in(arg_keys[1], 1), TOKENS // TOK_DEV)
    expert_ids_turns = jax.random.permutation(jax.random.fold_in(arg_keys[1], 3), TOKENS // TOK_DEV)
    expert_ids = jax.vmap(lambda own, number: routed_block(jax.random.fold_in(arg_keys[1], 2), own, number, TOK_DEV, EXPERTS, TOP, CAP, 2))(expert_ids_keys, expert_ids_turns).reshape((TOKENS, TOP))
    route_weight = jnp.clip(jnp.exp(math.log(1.0) - 2.3025851 * jax.random.uniform(arg_keys[2], (TOKENS, TOP), jnp.float32) ** steps_of(arg_keys[2], (TOKENS, TOP), ((0, 128),), -0.2, 0.2)), 0.1, 1.0)
    gate_weight = noise(arg_keys[3], (EXPERTS, FF, D), D ** -0.5, 0.09375, ((0, 64), (1, 2)))
    up_weight = noise(arg_keys[4], (EXPERTS, FF, D), D ** -0.5, 0.09375, ((0, 64), (1, 2)))
    down_weight = noise(arg_keys[5], (EXPERTS, FF, D), FF ** -0.5, 0.21875, ((0, 64), (2, 2)))
    return dict(tokens=tokens, expert_ids=expert_ids, route_weight=route_weight, gate_weight=gate_weight, up_weight=up_weight, down_weight=down_weight)


def reference(tokens, expert_ids, route_weight, gate_weight, up_weight, down_weight):
    blocks_count = N_FSDP * N_EXPERT
    per_block = TOK_DEV * TOP
    flat_ids = expert_ids.reshape(blocks_count, per_block).astype(jnp.int32)
    onehot = (flat_ids[:, :, None] == jnp.arange(EXPERTS, dtype=jnp.int32)[None, None, :]).astype(jnp.int32)
    rank_of = jnp.cumsum(onehot, axis=1) - onehot
    slot_of = jnp.sum(rank_of * onehot, axis=2).astype(jnp.int32)
    block_no = jnp.broadcast_to(jnp.arange(blocks_count, dtype=jnp.int32)[:, None], (blocks_count, per_block))
    token_no = block_no * TOK_DEV + jnp.arange(per_block, dtype=jnp.int32)[None, :] // TOP
    slot_tokens = jnp.full((EXPERTS, blocks_count, CAP), TOKENS, jnp.int32).at[flat_ids, block_no, slot_of].set(token_no)
    slot_weights = jnp.zeros((EXPERTS, blocks_count, CAP), jnp.float32).at[flat_ids, block_no, slot_of].set(
        route_weight.reshape(blocks_count, per_block).astype(jnp.float32))
    padded = jnp.concatenate([tokens, jnp.zeros((1, D), tokens.dtype)], axis=0)

    def per_expert(totals, inputs):
        gate_one, up_one, down_one, index_list, weight_list = inputs
        index_flat = index_list.reshape(-1)
        picked = padded[index_flat]
        gate_part = jnp.dot(picked, gate_one.T, preferred_element_type=jnp.float32)
        up_part = jnp.dot(picked, up_one.T, preferred_element_type=jnp.float32)
        hidden = (jax.nn.silu(gate_part) * up_part).astype(jnp.bfloat16)
        outputs = jnp.dot(hidden, down_one, preferred_element_type=jnp.float32).astype(jnp.bfloat16)
        totals = totals.at[index_flat].add(weight_list.reshape(-1)[:, None] * outputs.astype(jnp.float32))
        return totals, None

    totals, unused = lax.scan(per_expert, jnp.zeros((TOKENS + 1, D), jnp.float32),
                              (gate_weight, up_weight, down_weight, slot_tokens, slot_weights))
    return totals[:TOKENS].astype(jnp.bfloat16)
```

```python
import jax
import jax.numpy as jnp
from jax import lax
from jax.sharding import PartitionSpec as P

LANES = 128
CUTS = (0, 4, 9)


def routing_tables(expert_ids, experts_count):
    tok_count, top_count = expert_ids.shape
    names = jnp.arange(experts_count, dtype=jnp.int32)
    chosen = (expert_ids[:, :, None] == names[None, None, :]).astype(jnp.float32)
    by_token = jnp.sum(chosen, axis=1)
    earlier = jnp.arange(tok_count)[:, None] > jnp.arange(tok_count)[None, :]
    rank_of = jnp.dot(earlier.astype(jnp.bfloat16), by_token.astype(jnp.bfloat16),
                      preferred_element_type=jnp.float32)
    return by_token, rank_of


def swap_join(part, axis):
    other = lax.ppermute(part, "fsdp", [(0, 1), (1, 0)])
    first = lax.axis_index("fsdp") == 0
    return jnp.concatenate(
        [jnp.where(first, part, other), jnp.where(first, other, part)], axis=axis)


def body(tokens, expert_ids, route_weight, gate_weight, up_weight, down_weight):
    experts_count = lax.axis_size("expert") * gate_weight.shape[0]
    tok_count, top_count = expert_ids.shape
    width = tokens.shape[1]
    gate_full = swap_join(gate_weight[0], 0)
    up_full = swap_join(up_weight[0], 0)
    down_full = swap_join(down_weight[0], 1)
    by_token, rank_of = routing_tables(expert_ids, experts_count)
    names = jnp.arange(experts_count, dtype=jnp.int32)
    share = jnp.sum(
        jnp.where(expert_ids[:, :, None] == names, route_weight[:, :, None], 0.0), axis=1)

    def table(values, low, high):
        slots = jnp.arange(low, high, dtype=jnp.float32)
        hit = (rank_of[:, :, None] == slots) & (by_token[:, :, None] > 0)
        return jnp.where(hit, values[:, :, None], 0.0).reshape(tok_count, -1).astype(jnp.bfloat16)

    def exchange(rows, count):
        sent = rows.reshape(experts_count, count * width // LANES, LANES)
        came = lax.all_to_all(sent, "expert", split_axis=0, concat_axis=0, tiled=True)
        return came.reshape(experts_count * count, width)

    def dispatch(low, high):
        picker = table(jnp.ones_like(by_token), low, high)
        rows = jnp.einsum("tj,td->jd", picker, tokens,
                          preferred_element_type=jnp.float32).astype(jnp.bfloat16)
        return exchange(rows, high - low)

    def expert(rows):
        gate = jnp.einsum("sd,fd->sf", rows, gate_full, preferred_element_type=jnp.float32)
        up = jnp.einsum("sd,fd->sf", rows, up_full, preferred_element_type=jnp.float32)
        hidden = (jax.nn.silu(gate) * up).astype(jnp.bfloat16)
        return jnp.dot(hidden, down_full,
                       preferred_element_type=jnp.float32).astype(jnp.bfloat16)

    spans = list(zip(CUTS[:-1], CUTS[1:]))
    arrived = [dispatch(low, high) for low, high in spans]
    total = jnp.zeros((tok_count, width), jnp.float32)
    for (low, high), rows in zip(spans, arrived):
        back = exchange(expert(rows), high - low)
        total = total + jnp.dot(table(share, low, high), back, preferred_element_type=jnp.float32)
    return total.astype(jnp.bfloat16)


def solution(mesh):
    placed = (
        P(("fsdp", "expert"), None),
        P(("fsdp", "expert"), None),
        P(("fsdp", "expert"), None),
        P("expert", "fsdp", None),
        P("expert", "fsdp", None),
        P("expert", None, "fsdp"),
    )
    return jax.shard_map(
        body, mesh=mesh, in_specs=placed, out_specs=P(("fsdp", "expert"), None), check_vma=False
    )
```

```python
import functools

import jax
import jax.numpy as jnp
from jax import lax
from jax.experimental import pallas as pl
from jax.experimental.pallas import tpu as pltpu
from jax.sharding import PartitionSpec as P

LANES = 128
ROW_BLOCK = 64
FF_BLOCK = 256
COLUMN_BLOCK = 2048
STAGGER = 530
VMEM_LIMIT = 60 * 1024 * 1024


def dispatch_kernel(capacity, late_ref, ids_ref, tokens_ref, out_ref, place_ref,
                    rows_ref, spin_ref, where_ref, sem):
    top_count, tok_count = ids_ref.shape
    experts_count = out_ref.shape[0] // capacity
    parts = out_ref.shape[1]
    ids = ids_ref[...]
    name = lax.broadcasted_iota(jnp.int32, (experts_count, tok_count), 0)
    chosen = jnp.zeros((experts_count, tok_count), jnp.float32)
    for k in range(top_count):
        chosen += (ids[k:k + 1] == name).astype(jnp.float32)
    earlier = (lax.broadcasted_iota(jnp.int32, (tok_count, tok_count), 0)
               < lax.broadcasted_iota(jnp.int32, (tok_count, tok_count), 1))
    rank = jnp.dot(chosen.astype(jnp.bfloat16),
                   earlier.astype(jnp.float32).astype(jnp.bfloat16),
                   preferred_element_type=jnp.float32)
    start = rank + (name * capacity).astype(jnp.float32)
    place_ref[...] = jnp.zeros_like(place_ref)
    for k in range(top_count):
        place = jnp.sum(jnp.where(ids[k:k + 1] == name, start, 0.0), axis=0, keepdims=True)
        place_ref[k:k + 1, :tok_count] = place.astype(jnp.int32)
    copy = pltpu.make_async_copy(place_ref, where_ref, sem)
    copy.start()
    for part in range(parts):
        rows_ref[pl.ds(part, tok_count, stride=parts), :] = (
            tokens_ref[:, part * LANES:(part + 1) * LANES].astype(jnp.float32))
    spin_ref[...] = lax.fori_loop(
        0, late_ref[0], lambda i, a: jnp.sin(a) * 0.5 + 1.0, jnp.ones((8, LANES), jnp.float32))
    copy.wait()

    @pl.loop(0, tok_count)
    def _(t):
        first = pl.multiple_of(t * parts, parts)
        row = rows_ref[pl.ds(first, parts), :].astype(out_ref.dtype)
        for k in range(top_count):
            out_ref[where_ref[k, t]] = row


def dispatch(late, ids, tokens, experts_count, capacity):
    top_count, tok_count = ids.shape
    parts = tokens.shape[1] // LANES
    vmem = pl.BlockSpec(memory_space=pltpu.VMEM)
    smem = pl.BlockSpec(memory_space=pltpu.SMEM)
    return pl.pallas_call(
        functools.partial(dispatch_kernel, capacity),
        out_shape=(
            jax.ShapeDtypeStruct((experts_count * capacity, parts, LANES), tokens.dtype),
            jax.ShapeDtypeStruct((top_count, LANES), jnp.int32),
        ),
        in_specs=[smem, vmem, vmem],
        out_specs=(vmem, vmem),
        scratch_shapes=[
            pltpu.VMEM((tok_count * parts, LANES), jnp.float32),
            pltpu.VMEM((8, LANES), jnp.float32),
            pltpu.SMEM((top_count, LANES), jnp.int32),
            pltpu.SemaphoreType.DMA,
        ],
        compiler_params=pltpu.CompilerParams(vmem_limit_bytes=VMEM_LIMIT),
        name="dispatch",
    )(late, ids, tokens)


def expert_kernel(ff_steps, came_ref, gate_ref, up_ref, down_ref, out_ref,
                  wide_ref, rows_ref, hidden_ref, result_ref):
    step = pl.program_id(0)
    count, parts = came_ref.shape[0], came_ref.shape[1]
    out_parts = out_ref.shape[1]

    @pl.when(step == 0)
    def _():
        @pl.loop(0, count // ROW_BLOCK)
        def _(b):
            at = pl.multiple_of(b * ROW_BLOCK, ROW_BLOCK)
            block = came_ref[pl.ds(at, ROW_BLOCK)].astype(jnp.float32)
            wide_ref[...] = block.reshape(ROW_BLOCK * parts, LANES)
            for part in range(parts):
                rows_ref[pl.ds(at, ROW_BLOCK), part * LANES:(part + 1) * LANES] = (
                    wide_ref[pl.ds(part, ROW_BLOCK, stride=parts), :].astype(rows_ref.dtype))

    @pl.when(step < ff_steps)
    def _():
        contract = (((1,), (1,)), ((), ()))
        rows = rows_ref[...]
        gate = lax.dot_general(rows, gate_ref[...], contract, preferred_element_type=jnp.float32)
        up = lax.dot_general(rows, up_ref[...], contract, preferred_element_type=jnp.float32)
        hidden = gate / (1.0 + jnp.exp(-gate)) * up
        at = pl.multiple_of(step * FF_BLOCK, FF_BLOCK)
        hidden_ref[:, pl.ds(at, FF_BLOCK)] = hidden.astype(hidden_ref.dtype)

    @pl.when(step >= ff_steps)
    def _():
        hidden = hidden_ref[...]
        for piece in range(COLUMN_BLOCK // 256):
            result = jnp.dot(hidden, down_ref[:, piece * 256:(piece + 1) * 256],
                             preferred_element_type=jnp.float32)
            for half in range(2):
                result_ref[pl.ds(2 * piece + half, count, stride=out_parts), :] = (
                    result[:, half * LANES:(half + 1) * LANES])

        @pl.loop(0, count // ROW_BLOCK)
        def _(b):
            at = pl.multiple_of(b * ROW_BLOCK, ROW_BLOCK)
            first = pl.multiple_of(b * ROW_BLOCK * out_parts, ROW_BLOCK * out_parts)
            block = result_ref[pl.ds(first, ROW_BLOCK * out_parts), :]
            out_ref[pl.ds(at, ROW_BLOCK)] = block.reshape(
                ROW_BLOCK, out_parts, LANES).astype(out_ref.dtype)


def expert(came, gate, up, down):
    count, parts, _ = came.shape
    ff, width = gate.shape
    ff_steps, column_steps = ff // FF_BLOCK, width // COLUMN_BLOCK
    out_parts = COLUMN_BLOCK // LANES
    return pl.pallas_call(
        functools.partial(expert_kernel, ff_steps),
        out_shape=jax.ShapeDtypeStruct(came.shape, came.dtype),
        grid=(ff_steps + column_steps,),
        in_specs=[
            pl.BlockSpec((count, parts, LANES), lambda i: (0, 0, 0),
                         pipeline_mode=pl.Buffered(1)),
            pl.BlockSpec((FF_BLOCK, width), lambda i: (jnp.minimum(i, ff_steps - 1), 0)),
            pl.BlockSpec((FF_BLOCK, width), lambda i: (jnp.minimum(i, ff_steps - 1), 0)),
            pl.BlockSpec((ff, COLUMN_BLOCK), lambda i: (0, jnp.maximum(i - ff_steps, 0))),
        ],
        out_specs=pl.BlockSpec((count, out_parts, LANES),
                               lambda i: (0, jnp.maximum(i - ff_steps, 0), 0)),
        scratch_shapes=[
            pltpu.VMEM((ROW_BLOCK * parts, LANES), jnp.float32),
            pltpu.VMEM((count, width), came.dtype),
            pltpu.VMEM((count, ff), came.dtype),
            pltpu.VMEM((count * out_parts, LANES), jnp.float32),
        ],
        compiler_params=pltpu.CompilerParams(vmem_limit_bytes=VMEM_LIMIT),
        cost_estimate=pl.CostEstimate(
            flops=6 * count * ff * width, transcendentals=count * ff,
            bytes_accessed=2 * (3 * ff * width + 2 * count * width)),
        name="expert",
    )(came, gate, up, down)


def combine_kernel(place_ref, share_ref, back_ref, out_ref, total_ref):
    top_count, tok_count = share_ref.shape
    parts = back_ref.shape[1]

    @pl.loop(0, tok_count)
    def _(t):
        total = jnp.zeros((parts, LANES), jnp.float32)
        for k in range(top_count):
            total += share_ref[k, t] * back_ref[place_ref[k, t]].astype(jnp.float32)
        total_ref[pl.ds(pl.multiple_of(t * parts, parts), parts), :] = total

    for part in range(parts):
        out_ref[:, part * LANES:(part + 1) * LANES] = (
            total_ref[pl.ds(part, tok_count, stride=parts), :].astype(out_ref.dtype))


def combine(place, share, back):
    tok_count = share.shape[1]
    count, parts, _ = back.shape
    step_parts = parts // 2
    smem = pl.BlockSpec(memory_space=pltpu.SMEM)
    return pl.pallas_call(
        combine_kernel,
        out_shape=jax.ShapeDtypeStruct((tok_count, parts * LANES), back.dtype),
        grid=(2,),
        in_specs=[smem, smem,
                  pl.BlockSpec((count, step_parts, LANES), lambda i: (0, i, 0))],
        out_specs=pl.BlockSpec((tok_count, step_parts * LANES), lambda i: (0, i)),
        scratch_shapes=[pltpu.VMEM((tok_count * step_parts, LANES), jnp.float32)],
        compiler_params=pltpu.CompilerParams(vmem_limit_bytes=VMEM_LIMIT),
        name="combine",
    )(place, share, back)


def swap_join(part, axis):
    other = lax.ppermute(part, "fsdp", [(0, 1), (1, 0)])
    first = lax.axis_index("fsdp") == 0
    return jnp.concatenate(
        [jnp.where(first, part, other), jnp.where(first, other, part)], axis=axis)


def exchange(rows, experts_count):
    sent = rows.reshape(experts_count, -1, LANES)
    came = lax.all_to_all(sent, "expert", split_axis=0, concat_axis=0, tiled=True)
    return came.reshape(rows.shape)


def body(tokens, expert_ids, route_weight, gate_weight, up_weight, down_weight):
    experts_count = lax.axis_size("expert") * gate_weight.shape[0]
    tok_count, top_count = expert_ids.shape
    capacity = tok_count * top_count // experts_count + 1
    late = (lax.axis_index("fsdp") * STAGGER).astype(jnp.int32).reshape(1)
    sent, place = dispatch(late, expert_ids.T, tokens, experts_count, capacity)
    came = exchange(sent, experts_count)
    gate_full = swap_join(gate_weight[0], 0)
    up_full = swap_join(up_weight[0], 0)
    down_full = swap_join(down_weight[0], 1)
    back = exchange(expert(came, gate_full, up_full, down_full), experts_count)
    return combine(place, route_weight.T, back)


def solution(mesh):
    placed = (
        P(("fsdp", "expert"), None),
        P(("fsdp", "expert"), None),
        P(("fsdp", "expert"), None),
        P("expert", "fsdp", None),
        P("expert", "fsdp", None),
        P("expert", None, "fsdp"),
    )
    return jax.shard_map(
        body, mesh=mesh, in_specs=placed, out_specs=P(("fsdp", "expert"), None), check_vma=False
    )
```

```python
import functools

import jax
import jax.numpy as jnp
from jax import lax
from jax.experimental import pallas as pl
from jax.experimental.pallas import tpu as pltpu
from jax.sharding import PartitionSpec as P

LANES = 128
ROW_BLOCK = 64
FF_BLOCK = 128
COLUMN_BLOCK = 2048
STAGGER = 530
EXPERT_GROUP = 8
DISPATCH_LIMIT = 60 * 1024 * 1024
SMALL_LIMIT = 14 * 1024 * 1024
EXPERT_LIMIT = 48 * 1024 * 1024


def padded(parts):
    return parts + 8


def dispatch_kernel(capacity, late_ref, ids_ref, tokens_ref, out_ref, place_ref,
                    wide_ref, rows_ref, stage_ref, table_ref, where_ref, table_sem, out_sem):
    top_count, tok_count = ids_ref.shape
    parts = rows_ref.shape[1]
    experts_count = out_ref.shape[0] // capacity
    pitch = padded(parts)
    ids = ids_ref[...]
    name = lax.broadcasted_iota(jnp.int32, (experts_count, tok_count), 0)
    token = lax.broadcasted_iota(jnp.int32, (experts_count, tok_count), 1)
    chosen = jnp.zeros((experts_count, tok_count), jnp.float32)
    for k in range(top_count):
        chosen += (ids[k:k + 1] == name).astype(jnp.float32)
    earlier = (lax.broadcasted_iota(jnp.int32, (tok_count, tok_count), 0)
               < lax.broadcasted_iota(jnp.int32, (tok_count, tok_count), 1))
    rank = jnp.dot(chosen.astype(jnp.bfloat16),
                   earlier.astype(jnp.float32).astype(jnp.bfloat16),
                   preferred_element_type=jnp.float32)
    held = jnp.where(chosen > 0.0, rank, -1.0)
    lane = lax.broadcasted_iota(jnp.int32, (experts_count, LANES), 1)
    table = jnp.zeros((experts_count, LANES), jnp.float32)
    for slot in range(capacity):
        source = jnp.sum(jnp.where(held == float(slot), token.astype(jnp.float32), 0.0),
                         axis=1, keepdims=True)
        table = jnp.where(lane == slot, source, table)
    table_ref[...] = table.astype(jnp.int32)
    copy = pltpu.make_async_copy(table_ref, where_ref, table_sem)
    copy.start()
    place_ref[...] = lax.fori_loop(
        0, late_ref[0], lambda i, a: jnp.sin(a) * 0.5 + 1.0,
        jnp.ones(place_ref.shape, jnp.float32)).astype(jnp.int32)
    start = rank + (name * capacity).astype(jnp.float32)
    for k in range(top_count):
        place = jnp.sum(jnp.where(ids[k:k + 1] == name, start, 0.0), axis=0, keepdims=True)
        place_ref[k:k + 1, :tok_count] = place.astype(jnp.int32)
    for part in range(parts):
        wide_ref[pl.ds(part, tok_count, stride=pitch), :] = (
            tokens_ref[:, part * LANES:(part + 1) * LANES].astype(jnp.float32))
    for t in range(tok_count):
        rows_ref[t] = wide_ref[t * pitch:t * pitch + parts, :].astype(rows_ref.dtype)
    copy.wait()

    group = EXPERT_GROUP * capacity

    def send(g):
        at = pl.multiple_of(g * group, group)
        return pltpu.make_async_copy(stage_ref.at[pl.ds(at, group)],
                                     out_ref.at[pl.ds(at, group)], out_sem.at[g])

    @pl.loop(0, experts_count // EXPERT_GROUP)
    def _(g):
        @pl.loop(0, EXPERT_GROUP)
        def _(i):
            e = g * EXPERT_GROUP + i
            for slot in range(capacity):
                stage_ref[e * capacity + slot] = rows_ref[where_ref[e, slot]]
        send(g).start()

    @pl.loop(0, experts_count // EXPERT_GROUP)
    def _(g):
        send(g).wait()


def dispatch(late, ids, tokens, experts_count, capacity):
    top_count, tok_count = ids.shape
    parts = tokens.shape[1] // LANES
    count = experts_count * capacity
    vmem = pl.BlockSpec(memory_space=pltpu.VMEM)
    smem = pl.BlockSpec(memory_space=pltpu.SMEM)
    return pl.pallas_call(
        functools.partial(dispatch_kernel, capacity),
        out_shape=(
            jax.ShapeDtypeStruct((count, parts, LANES), tokens.dtype),
            jax.ShapeDtypeStruct((top_count, LANES), jnp.int32),
        ),
        in_specs=[smem, vmem, vmem],
        out_specs=(pl.BlockSpec(memory_space=pltpu.HBM), vmem),
        scratch_shapes=[
            pltpu.VMEM((tok_count * padded(parts), LANES), jnp.float32),
            pltpu.VMEM((tok_count, parts, LANES), tokens.dtype),
            pltpu.VMEM((count, parts, LANES), tokens.dtype),
            pltpu.VMEM((experts_count, LANES), jnp.int32),
            pltpu.SMEM((experts_count, LANES), jnp.int32),
            pltpu.SemaphoreType.DMA,
            pltpu.SemaphoreType.DMA((experts_count // EXPERT_GROUP,)),
        ],
        compiler_params=pltpu.CompilerParams(vmem_limit_bytes=DISPATCH_LIMIT),
        name="dispatch",
    )(late, ids, tokens)


def settle_kernel(gate_ref, up_ref, down_ref, gate_out_ref, up_out_ref, down_out_ref):
    del gate_ref, up_ref, down_ref, gate_out_ref, up_out_ref, down_out_ref


def partner_weights(parts):
    others = [lax.ppermute(part, "fsdp", [(0, 1), (1, 0)]) for part in parts]
    hbm = pl.BlockSpec(memory_space=pltpu.HBM)
    return pl.pallas_call(
        settle_kernel,
        out_shape=tuple(jax.ShapeDtypeStruct(part.shape, part.dtype) for part in others),
        in_specs=[hbm] * 3,
        out_specs=(hbm,) * 3,
        input_output_aliases={0: 0, 1: 1, 2: 2},
        cost_estimate=pl.CostEstimate(
            flops=10**11, transcendentals=0, bytes_accessed=4 * 10**8),
        name="settle",
    )(*others)


def expert_kernel(came_ref, gate_ref, up_ref, down_ref, gate_other_ref, up_other_ref,
                  down_other_ref, out_ref, held_ref, gate_all_ref, up_all_ref, down_all_ref,
                  wide_ref, rows_ref, hidden_ref, result_ref, came_sem, gate_sem, up_sem,
                  down_sem):
    count, parts = came_ref.shape[0], came_ref.shape[1]
    half_ff, width = gate_ref.shape
    columns = down_ref.shape[1]
    pitch = padded(parts)
    mine = lax.axis_index("fsdp")

    def fetch(b):
        at = pl.multiple_of(b * ROW_BLOCK, ROW_BLOCK)
        return pltpu.make_async_copy(came_ref.at[pl.ds(at, ROW_BLOCK)],
                                     held_ref.at[pl.ds(at, ROW_BLOCK)], came_sem.at[b])

    @pl.loop(0, count // ROW_BLOCK)
    def _(b):
        fetch(b).start()

    gate_copies, up_copies = [], []
    for low in range(0, 2 * half_ff, FF_BLOCK):
        own = low < half_ff
        at = low % half_ff
        step = low // FF_BLOCK
        gate_copies.append(pltpu.make_async_copy(
            (gate_ref if own else gate_other_ref).at[at:at + FF_BLOCK],
            gate_all_ref.at[low:low + FF_BLOCK], gate_sem.at[step]))
        up_copies.append(pltpu.make_async_copy(
            (up_ref if own else up_other_ref).at[at:at + FF_BLOCK],
            up_all_ref.at[low:low + FF_BLOCK], up_sem.at[step]))
        gate_copies[-1].start()
        up_copies[-1].start()
    down_copies = []
    for which, (part, index) in enumerate(((down_ref, mine), (down_other_ref, 1 - mine))):
        to = pl.multiple_of(index * columns, columns)
        for half, owner in enumerate((mine, 1 - mine)):
            at = pl.multiple_of(owner * half_ff, half_ff)
            down_copies.append(pltpu.make_async_copy(
                part.at[pl.ds(at, half_ff)],
                down_all_ref.at[half * half_ff:(half + 1) * half_ff, pl.ds(to, columns)],
                down_sem.at[2 * which + half]))
            down_copies[-1].start()

    @pl.loop(0, count // ROW_BLOCK)
    def _(b):
        fetch(b).wait()
        at = pl.multiple_of(b * ROW_BLOCK, ROW_BLOCK)
        for row in range(ROW_BLOCK):
            wide_ref[row * pitch:row * pitch + parts, :] = held_ref[at + row].astype(jnp.float32)
        for part in range(parts):
            rows_ref[pl.ds(at, ROW_BLOCK), part * LANES:(part + 1) * LANES] = (
                wide_ref[pl.ds(part, ROW_BLOCK, stride=pitch), :].astype(rows_ref.dtype))

    contract = (((1,), (1,)), ((), ()))
    for step, low in enumerate(range(0, 2 * half_ff, FF_BLOCK)):
        gate_copies[step].wait()
        up_copies[step].wait()
        rows = rows_ref[...]
        gate = lax.dot_general(rows, gate_all_ref[low:low + FF_BLOCK], contract,
                               preferred_element_type=jnp.float32)
        up = lax.dot_general(rows, up_all_ref[low:low + FF_BLOCK], contract,
                             preferred_element_type=jnp.float32)
        hidden = gate / (1.0 + jnp.exp(-gate)) * up
        hidden_ref[:, low:low + FF_BLOCK] = hidden.astype(hidden_ref.dtype)
    for copy in down_copies:
        copy.wait()

    out_parts = COLUMN_BLOCK // LANES
    out_pitch = padded(out_parts)
    for block in range(width // COLUMN_BLOCK):
        for piece in range(COLUMN_BLOCK // 256):
            low = block * COLUMN_BLOCK + piece * 256
            result = jnp.dot(hidden_ref[...], down_all_ref[:, low:low + 256],
                             preferred_element_type=jnp.float32)
            for half in range(2):
                result_ref[pl.ds(2 * piece + half, count, stride=out_pitch), :] = (
                    result[:, half * LANES:(half + 1) * LANES])

        @pl.loop(0, count // ROW_BLOCK)
        def _(b):
            at = pl.multiple_of(b * ROW_BLOCK, ROW_BLOCK)
            for row in range(ROW_BLOCK):
                first = pl.multiple_of((at + row) * out_pitch, 8)
                out_ref[at + row, block * out_parts:(block + 1) * out_parts] = (
                    result_ref[pl.ds(first, out_parts), :].astype(out_ref.dtype))


def expert(came, own, other):
    count, parts, _ = came.shape
    half_ff, width = own[0].shape
    ff, dtype = 2 * half_ff, came.dtype
    steps = ff // FF_BLOCK
    anywhere = pl.BlockSpec(memory_space=pl.ANY)
    return pl.pallas_call(
        expert_kernel,
        out_shape=jax.ShapeDtypeStruct(came.shape, dtype),
        in_specs=[anywhere] * 7,
        out_specs=pl.BlockSpec(memory_space=pltpu.VMEM),
        scratch_shapes=[
            pltpu.VMEM(came.shape, dtype),
            pltpu.VMEM((ff, width), dtype),
            pltpu.VMEM((ff, width), dtype),
            pltpu.VMEM((ff, width), dtype),
            pltpu.VMEM((ROW_BLOCK * padded(parts), LANES), jnp.float32),
            pltpu.VMEM((count, width), dtype),
            pltpu.VMEM((count, ff), dtype),
            pltpu.VMEM((count * padded(COLUMN_BLOCK // LANES), LANES), jnp.float32),
            pltpu.SemaphoreType.DMA((count // ROW_BLOCK,)),
            pltpu.SemaphoreType.DMA((steps,)),
            pltpu.SemaphoreType.DMA((steps,)),
            pltpu.SemaphoreType.DMA((4,)),
        ],
        compiler_params=pltpu.CompilerParams(vmem_limit_bytes=EXPERT_LIMIT),
        cost_estimate=pl.CostEstimate(
            flops=6 * count * ff * width, transcendentals=count * ff,
            bytes_accessed=2 * (3 * ff * width + 2 * count * width)),
        name="expert",
    )(came, *own, *other)


def combine_kernel(place_ref, share_ref, back_ref, out_ref, total_ref):
    top_count, tok_count = share_ref.shape
    parts = back_ref.shape[1]
    pitch = padded(parts)

    @pl.loop(0, tok_count)
    def _(t):
        total = jnp.zeros((parts, LANES), jnp.float32)
        for k in range(top_count):
            total += share_ref[k, t] * back_ref[place_ref[k, t]].astype(jnp.float32)
        total_ref[pl.ds(pl.multiple_of(t * pitch, 8), parts), :] = total

    for part in range(parts):
        out_ref[:, part * LANES:(part + 1) * LANES] = (
            total_ref[pl.ds(part, tok_count, stride=pitch), :].astype(out_ref.dtype))


def combine(place, share, back):
    tok_count = share.shape[1]
    parts = back.shape[1]
    smem = pl.BlockSpec(memory_space=pltpu.SMEM)
    vmem = pl.BlockSpec(memory_space=pltpu.VMEM)
    return pl.pallas_call(
        combine_kernel,
        out_shape=jax.ShapeDtypeStruct((tok_count, parts * LANES), back.dtype),
        in_specs=[smem, smem, vmem],
        out_specs=vmem,
        scratch_shapes=[pltpu.VMEM((tok_count * padded(parts), LANES), jnp.float32)],
        compiler_params=pltpu.CompilerParams(vmem_limit_bytes=SMALL_LIMIT),
        name="combine",
    )(place, share, back)


def exchange(rows, experts_count):
    sent = rows.reshape(experts_count, -1, LANES)
    came = lax.all_to_all(sent, "expert", split_axis=0, concat_axis=0, tiled=True)
    return came.reshape(rows.shape)


def body(tokens, expert_ids, route_weight, gate_weight, up_weight, down_weight):
    experts_count = lax.axis_size("expert") * gate_weight.shape[0]
    tok_count, top_count = expert_ids.shape
    capacity = tok_count * top_count // experts_count + 1
    late = (lax.axis_index("fsdp") * STAGGER).astype(jnp.int32).reshape(1)
    sent, place = dispatch(late, expert_ids.T, tokens, experts_count, capacity)
    came = exchange(sent, experts_count)
    own = (gate_weight[0], up_weight[0], down_weight[0])
    back = exchange(expert(came, own, partner_weights(own)), experts_count)
    return combine(place, route_weight.T, back)


def solution(mesh):
    placed = (
        P(("fsdp", "expert"), None),
        P(("fsdp", "expert"), None),
        P(("fsdp", "expert"), None),
        P("expert", "fsdp", None),
        P("expert", "fsdp", None),
        P("expert", None, "fsdp"),
    )
    return jax.shard_map(
        body, mesh=mesh, in_specs=placed, out_specs=P(("fsdp", "expert"), None), check_vma=False
    )
```

```python
import functools

import jax
import jax.numpy as jnp
from jax import lax
from jax.experimental import pallas as pl
from jax.experimental.pallas import tpu as pltpu
from jax.sharding import PartitionSpec as P

LANES = 128
ROW_BLOCK = 64
FF_BLOCK = 256
PIECE = 128
COLUMN_BLOCK = 2048
STAGGER = 700
EXPERT_GROUP = 8
DISPATCH_LIMIT = 60 * 1024 * 1024
SMALL_LIMIT = 14 * 1024 * 1024
EXPERT_LIMIT = 48 * 1024 * 1024


def padded(parts):
    return parts + 8


def dispatch_kernel(capacity, late_ref, ids_ref, tokens_ref, out_ref, place_ref,
                    wide_ref, rows_ref, stage_ref, table_ref, where_ref, table_sem, out_sem):
    top_count, tok_count = ids_ref.shape
    parts = rows_ref.shape[1]
    experts_count = out_ref.shape[0] // capacity
    pitch = padded(parts)
    ids = ids_ref[...]
    name = lax.broadcasted_iota(jnp.int32, (experts_count, tok_count), 0)
    token = lax.broadcasted_iota(jnp.int32, (experts_count, tok_count), 1)
    chosen = jnp.zeros((experts_count, tok_count), jnp.float32)
    for k in range(top_count):
        chosen += (ids[k:k + 1] == name).astype(jnp.float32)
    earlier = (lax.broadcasted_iota(jnp.int32, (tok_count, tok_count), 0)
               < lax.broadcasted_iota(jnp.int32, (tok_count, tok_count), 1))
    rank = jnp.dot(chosen.astype(jnp.bfloat16),
                   earlier.astype(jnp.float32).astype(jnp.bfloat16),
                   preferred_element_type=jnp.float32)
    held = jnp.where(chosen > 0.0, rank, -1.0)
    lane = lax.broadcasted_iota(jnp.int32, (experts_count, LANES), 1)
    table = jnp.zeros((experts_count, LANES), jnp.float32)
    for slot in range(capacity):
        source = jnp.sum(jnp.where(held == float(slot), token.astype(jnp.float32), 0.0),
                         axis=1, keepdims=True)
        table = jnp.where(lane == slot, source, table)
    table_ref[...] = table.astype(jnp.int32)
    copy = pltpu.make_async_copy(table_ref, where_ref, table_sem)
    copy.start()
    place_ref[...] = lax.fori_loop(
        0, late_ref[0], lambda i, a: jnp.sin(a) * 0.5 + 1.0,
        jnp.ones(place_ref.shape, jnp.float32)).astype(jnp.int32)
    start = rank + (name * capacity).astype(jnp.float32)
    for k in range(top_count):
        place = jnp.sum(jnp.where(ids[k:k + 1] == name, start, 0.0), axis=0, keepdims=True)
        place_ref[k:k + 1, :tok_count] = place.astype(jnp.int32)
    for part in range(parts):
        wide_ref[pl.ds(part, tok_count, stride=pitch), :] = (
            tokens_ref[:, part * LANES:(part + 1) * LANES].astype(jnp.float32))
    for t in range(tok_count):
        rows_ref[t] = wide_ref[t * pitch:t * pitch + parts, :].astype(rows_ref.dtype)
    copy.wait()

    group = EXPERT_GROUP * capacity

    def send(g):
        at = pl.multiple_of(g * group, group)
        return pltpu.make_async_copy(stage_ref.at[pl.ds(at, group)],
                                     out_ref.at[pl.ds(at, group)], out_sem.at[g])

    @pl.loop(0, experts_count // EXPERT_GROUP)
    def _(g):
        @pl.loop(0, EXPERT_GROUP)
        def _(i):
            e = g * EXPERT_GROUP + i
            for slot in range(capacity):
                stage_ref[e * capacity + slot] = rows_ref[where_ref[e, slot]]
        send(g).start()

    @pl.loop(0, experts_count // EXPERT_GROUP)
    def _(g):
        send(g).wait()


def dispatch(late, ids, tokens, experts_count, capacity):
    top_count, tok_count = ids.shape
    parts = tokens.shape[1] // LANES
    count = experts_count * capacity
    vmem = pl.BlockSpec(memory_space=pltpu.VMEM)
    smem = pl.BlockSpec(memory_space=pltpu.SMEM)
    return pl.pallas_call(
        functools.partial(dispatch_kernel, capacity),
        out_shape=(
            jax.ShapeDtypeStruct((count, parts, LANES), tokens.dtype),
            jax.ShapeDtypeStruct((top_count, LANES), jnp.int32),
        ),
        in_specs=[smem, vmem, vmem],
        out_specs=(pl.BlockSpec(memory_space=pltpu.HBM), vmem),
        scratch_shapes=[
            pltpu.VMEM((tok_count * padded(parts), LANES), jnp.float32),
            pltpu.VMEM((tok_count, parts, LANES), tokens.dtype),
            pltpu.VMEM((count, parts, LANES), tokens.dtype),
            pltpu.VMEM((experts_count, LANES), jnp.int32),
            pltpu.SMEM((experts_count, LANES), jnp.int32),
            pltpu.SemaphoreType.DMA,
            pltpu.SemaphoreType.DMA((experts_count // EXPERT_GROUP,)),
        ],
        compiler_params=pltpu.CompilerParams(vmem_limit_bytes=DISPATCH_LIMIT),
        name="dispatch",
    )(late, ids, tokens)


def settle_kernel(gate_ref, up_ref, down_ref, gate_out_ref, up_out_ref, down_out_ref):
    del gate_ref, up_ref, down_ref, gate_out_ref, up_out_ref, down_out_ref


def partner_weights(parts):
    others = [lax.ppermute(part, "fsdp", [(0, 1), (1, 0)]) for part in parts]
    hbm = pl.BlockSpec(memory_space=pltpu.HBM)
    return pl.pallas_call(
        settle_kernel,
        out_shape=tuple(jax.ShapeDtypeStruct(part.shape, part.dtype) for part in others),
        in_specs=[hbm] * 3,
        out_specs=(hbm,) * 3,
        input_output_aliases={0: 0, 1: 1, 2: 2},
        cost_estimate=pl.CostEstimate(
            flops=10**11, transcendentals=0, bytes_accessed=4 * 10**8),
        name="settle",
    )(*others)


def expert_kernel(came_ref, gate_ref, up_ref, down_ref, gate_other_ref, up_other_ref,
                  down_other_ref, out_ref, held_ref, gate_all_ref, up_all_ref, down_all_ref,
                  wide_ref, rows_ref, hidden_ref, result_ref, came_sem, gate_sem, up_sem,
                  down_sem):
    count, parts = came_ref.shape[0], came_ref.shape[1]
    half_ff, width = gate_ref.shape
    columns = down_ref.shape[1]
    pitch = padded(parts)
    mine = lax.axis_index("fsdp")

    def fetch(b):
        at = pl.multiple_of(b * ROW_BLOCK, ROW_BLOCK)
        return pltpu.make_async_copy(came_ref.at[pl.ds(at, ROW_BLOCK)],
                                     held_ref.at[pl.ds(at, ROW_BLOCK)], came_sem.at[b])

    @pl.loop(0, count // ROW_BLOCK)
    def _(b):
        fetch(b).start()

    pairs = ((gate_ref, gate_other_ref, gate_all_ref, gate_sem),
             (up_ref, up_other_ref, up_all_ref, up_sem))
    pieces = []
    for low in range(0, 2 * half_ff, PIECE):
        at, own = low % half_ff, low < half_ff
        for first, second, full, sem in pairs:
            pieces.append(pltpu.make_async_copy(
                (first if own else second).at[at:at + PIECE],
                full.at[low:low + PIECE], sem.at[low // PIECE]))
    per_step = len(pairs) * FF_BLOCK // PIECE
    down_copies = []
    for which, (part, index) in enumerate(((down_ref, mine), (down_other_ref, 1 - mine))):
        to = pl.multiple_of(index * columns, columns)
        for half, owner in enumerate((mine, 1 - mine)):
            at = pl.multiple_of(owner * half_ff, half_ff)
            down_copies.append(pltpu.make_async_copy(
                part.at[pl.ds(at, half_ff)],
                down_all_ref.at[half * half_ff:(half + 1) * half_ff, pl.ds(to, columns)],
                down_sem.at[2 * which + half]))

    def relay(b):
        fetch(b).wait()
        at = pl.multiple_of(b * ROW_BLOCK, ROW_BLOCK)
        for row in range(ROW_BLOCK):
            wide_ref[row * pitch:row * pitch + parts, :] = held_ref[at + row].astype(jnp.float32)
        for part in range(parts):
            rows_ref[pl.ds(at, ROW_BLOCK), part * LANES:(part + 1) * LANES] = (
                wide_ref[pl.ds(part, ROW_BLOCK, stride=pitch), :].astype(rows_ref.dtype))

    blocks = count // ROW_BLOCK
    steps = 2 * half_ff // FF_BLOCK
    for step in range(steps):
        for copy in pieces[step * per_step:(step + 1) * per_step]:
            copy.start()
        pl.loop(step * blocks // steps, (step + 1) * blocks // steps)(relay)
    for copy in down_copies:
        copy.start()

    contract = (((1,), (1,)), ((), ()))
    for step in range(steps):
        for copy in pieces[step * per_step:(step + 1) * per_step]:
            copy.wait()
        low = step * FF_BLOCK
        rows = rows_ref[...]
        gate = lax.dot_general(rows, gate_all_ref[low:low + FF_BLOCK], contract,
                               preferred_element_type=jnp.float32)
        up = lax.dot_general(rows, up_all_ref[low:low + FF_BLOCK], contract,
                             preferred_element_type=jnp.float32)
        hidden = gate / (1.0 + jnp.exp(-gate)) * up
        hidden_ref[:, low:low + FF_BLOCK] = hidden.astype(hidden_ref.dtype)
    for copy in down_copies:
        copy.wait()

    out_parts = COLUMN_BLOCK // LANES
    out_pitch = padded(out_parts)
    for block in range(width // COLUMN_BLOCK):
        for piece in range(COLUMN_BLOCK // 256):
            low = block * COLUMN_BLOCK + piece * 256
            result = jnp.dot(hidden_ref[...], down_all_ref[:, low:low + 256],
                             preferred_element_type=jnp.float32)
            for half in range(2):
                result_ref[pl.ds(2 * piece + half, count, stride=out_pitch), :] = (
                    result[:, half * LANES:(half + 1) * LANES])

        @pl.loop(0, count // ROW_BLOCK)
        def _(b):
            at = pl.multiple_of(b * ROW_BLOCK, ROW_BLOCK)
            for row in range(ROW_BLOCK):
                first = pl.multiple_of((at + row) * out_pitch, 8)
                out_ref[at + row, block * out_parts:(block + 1) * out_parts] = (
                    result_ref[pl.ds(first, out_parts), :].astype(out_ref.dtype))


def expert(came, own, other):
    count, parts, _ = came.shape
    half_ff, width = own[0].shape
    ff, dtype = 2 * half_ff, came.dtype
    steps = ff // PIECE
    anywhere = pl.BlockSpec(memory_space=pl.ANY)
    return pl.pallas_call(
        expert_kernel,
        out_shape=jax.ShapeDtypeStruct(came.shape, dtype),
        in_specs=[anywhere] * 7,
        out_specs=pl.BlockSpec(memory_space=pltpu.VMEM),
        scratch_shapes=[
            pltpu.VMEM(came.shape, dtype),
            pltpu.VMEM((ff, width), dtype),
            pltpu.VMEM((ff, width), dtype),
            pltpu.VMEM((ff, width), dtype),
            pltpu.VMEM((ROW_BLOCK * padded(parts), LANES), jnp.float32),
            pltpu.VMEM((count, width), dtype),
            pltpu.VMEM((count, ff), dtype),
            pltpu.VMEM((count * padded(COLUMN_BLOCK // LANES), LANES), jnp.float32),
            pltpu.SemaphoreType.DMA((count // ROW_BLOCK,)),
            pltpu.SemaphoreType.DMA((steps,)),
            pltpu.SemaphoreType.DMA((steps,)),
            pltpu.SemaphoreType.DMA((4,)),
        ],
        compiler_params=pltpu.CompilerParams(vmem_limit_bytes=EXPERT_LIMIT),
        cost_estimate=pl.CostEstimate(
            flops=6 * count * ff * width, transcendentals=count * ff,
            bytes_accessed=2 * (3 * ff * width + 2 * count * width)),
        name="expert",
    )(came, *own, *other)


def combine_kernel(place_ref, share_ref, back_ref, out_ref, total_ref):
    top_count, tok_count = share_ref.shape
    parts = back_ref.shape[1]
    pitch = padded(parts)

    @pl.loop(0, tok_count)
    def _(t):
        total = jnp.zeros((parts, LANES), jnp.float32)
        for k in range(top_count):
            total += share_ref[k, t] * back_ref[place_ref[k, t]].astype(jnp.float32)
        total_ref[pl.ds(pl.multiple_of(t * pitch, 8), parts), :] = total

    for part in range(parts):
        out_ref[:, part * LANES:(part + 1) * LANES] = (
            total_ref[pl.ds(part, tok_count, stride=pitch), :].astype(out_ref.dtype))


def combine(place, share, back):
    tok_count = share.shape[1]
    parts = back.shape[1]
    smem = pl.BlockSpec(memory_space=pltpu.SMEM)
    vmem = pl.BlockSpec(memory_space=pltpu.VMEM)
    return pl.pallas_call(
        combine_kernel,
        out_shape=jax.ShapeDtypeStruct((tok_count, parts * LANES), back.dtype),
        in_specs=[smem, smem, vmem],
        out_specs=vmem,
        scratch_shapes=[pltpu.VMEM((tok_count * padded(parts), LANES), jnp.float32)],
        compiler_params=pltpu.CompilerParams(vmem_limit_bytes=SMALL_LIMIT),
        name="combine",
    )(place, share, back)


def exchange(rows, experts_count):
    sent = rows.reshape(experts_count, -1, LANES)
    came = lax.all_to_all(sent, "expert", split_axis=0, concat_axis=0, tiled=True)
    return came.reshape(rows.shape)


def body(tokens, expert_ids, route_weight, gate_weight, up_weight, down_weight):
    experts_count = lax.axis_size("expert") * gate_weight.shape[0]
    tok_count, top_count = expert_ids.shape
    capacity = tok_count * top_count // experts_count + 1
    late = (lax.axis_index("fsdp") * STAGGER).astype(jnp.int32).reshape(1)
    sent, place = dispatch(late, expert_ids.T, tokens, experts_count, capacity)
    came = exchange(sent, experts_count)
    own = (gate_weight[0], up_weight[0], down_weight[0])
    back = exchange(expert(came, own, partner_weights(own)), experts_count)
    return combine(place, route_weight.T, back)


def solution(mesh):
    placed = (
        P(("fsdp", "expert"), None),
        P(("fsdp", "expert"), None),
        P(("fsdp", "expert"), None),
        P("expert", "fsdp", None),
        P("expert", "fsdp", None),
        P("expert", None, "fsdp"),
    )
    return jax.shard_map(
        body, mesh=mesh, in_specs=placed, out_specs=P(("fsdp", "expert"), None), check_vma=False
    )
```

```python
import functools

import jax
import jax.numpy as jnp
from jax import lax
from jax.experimental import pallas as pl
from jax.experimental.pallas import tpu as pltpu
from jax.sharding import PartitionSpec as P

LANES = 128
ROW_BLOCK = 64
FF_BLOCK = 256
PIECE = 128
PRODUCT = 512
COLUMN_BLOCK = 2048
STAGGER = 696
EXPERT_GROUP = 4
DISPATCH_LIMIT = 60 * 1024 * 1024
SMALL_LIMIT = 14 * 1024 * 1024
EXPERT_LIMIT = 50 * 1024 * 1024


def padded(parts):
    return parts + 8


def dispatch_kernel(capacity, late_ref, ids_ref, tokens_ref, out_ref, place_ref,
                    wide_ref, rows_ref, stage_ref, table_ref, where_ref, table_sem, out_sem):
    top_count, tok_count = ids_ref.shape
    parts = rows_ref.shape[1]
    experts_count = out_ref.shape[0] // capacity
    pitch = padded(parts)
    ids = ids_ref[...]
    name = lax.broadcasted_iota(jnp.int32, (experts_count, tok_count), 0)
    token = lax.broadcasted_iota(jnp.int32, (experts_count, tok_count), 1)
    chosen = jnp.zeros((experts_count, tok_count), jnp.float32)
    for k in range(top_count):
        chosen += (ids[k:k + 1] == name).astype(jnp.float32)
    earlier = (lax.broadcasted_iota(jnp.int32, (tok_count, tok_count), 0)
               < lax.broadcasted_iota(jnp.int32, (tok_count, tok_count), 1))
    rank = jnp.dot(chosen.astype(jnp.bfloat16),
                   earlier.astype(jnp.float32).astype(jnp.bfloat16),
                   preferred_element_type=jnp.float32)
    held = jnp.where(chosen > 0.0, rank, -1.0)
    lane = lax.broadcasted_iota(jnp.int32, (experts_count, LANES), 1)
    table = jnp.zeros((experts_count, LANES), jnp.float32)
    for slot in range(capacity):
        source = jnp.sum(jnp.where(held == float(slot), token.astype(jnp.float32), 0.0),
                         axis=1, keepdims=True)
        table = jnp.where(lane == slot, source, table)
    table_ref[...] = table.astype(jnp.int32)
    copy = pltpu.make_async_copy(table_ref, where_ref, table_sem)
    copy.start()
    waited = lax.fori_loop(
        0, late_ref[0], lambda i, a: jnp.sin(a) * 0.5 + 1.0,
        jnp.ones(place_ref.shape, jnp.float32)).astype(jnp.int32)
    place_ref[...] = waited
    for part in range(parts):
        wide_ref[pl.ds(part, tok_count, stride=pitch), :] = (
            tokens_ref[:, part * LANES:(part + 1) * LANES].astype(jnp.float32))
    for t in range(tok_count):
        rows_ref[t] = wide_ref[t * pitch:t * pitch + parts, :].astype(rows_ref.dtype)
    copy.wait()

    group = EXPERT_GROUP * capacity

    def send(g):
        at = pl.multiple_of(g * group, group)
        return pltpu.make_async_copy(stage_ref.at[pl.ds(at, group)],
                                     out_ref.at[pl.ds(at, group)], out_sem.at[g])

    @pl.loop(0, experts_count // EXPERT_GROUP)
    def _(g):
        @pl.loop(0, EXPERT_GROUP, unroll=4)
        def _(i):
            e = g * EXPERT_GROUP + i
            for slot in range(capacity):
                stage_ref[e * capacity + slot] = rows_ref[where_ref[e, slot]]
        send(g).start()

    start = rank + (name * capacity).astype(jnp.float32)
    for k in range(top_count):
        place = jnp.sum(jnp.where(ids[k:k + 1] == name, start, 0.0), axis=0, keepdims=True)
        place_ref[k:k + 1, :tok_count] = place.astype(jnp.int32)

    @pl.loop(0, experts_count // EXPERT_GROUP)
    def _(g):
        send(g).wait()


def dispatch(late, ids, tokens, experts_count, capacity):
    top_count, tok_count = ids.shape
    parts = tokens.shape[1] // LANES
    count = experts_count * capacity
    vmem = pl.BlockSpec(memory_space=pltpu.VMEM)
    smem = pl.BlockSpec(memory_space=pltpu.SMEM)
    return pl.pallas_call(
        functools.partial(dispatch_kernel, capacity),
        out_shape=(
            jax.ShapeDtypeStruct((count, parts, LANES), tokens.dtype),
            jax.ShapeDtypeStruct((top_count, LANES), jnp.int32),
        ),
        in_specs=[smem, vmem, vmem],
        out_specs=(pl.BlockSpec(memory_space=pltpu.HBM), vmem),
        scratch_shapes=[
            pltpu.VMEM((tok_count * padded(parts), LANES), jnp.float32),
            pltpu.VMEM((tok_count, parts, LANES), tokens.dtype),
            pltpu.VMEM((count, parts, LANES), tokens.dtype),
            pltpu.VMEM((experts_count, LANES), jnp.int32),
            pltpu.SMEM((experts_count, LANES), jnp.int32),
            pltpu.SemaphoreType.DMA,
            pltpu.SemaphoreType.DMA((experts_count // EXPERT_GROUP,)),
        ],
        compiler_params=pltpu.CompilerParams(vmem_limit_bytes=DISPATCH_LIMIT),
        name="dispatch",
    )(late, ids, tokens)


def settle_kernel(gate_ref, up_ref, down_ref, gate_out_ref, up_out_ref, down_out_ref):
    del gate_ref, up_ref, down_ref, gate_out_ref, up_out_ref, down_out_ref


def partner_weights(parts):
    others = [lax.ppermute(part, "fsdp", [(0, 1), (1, 0)]) for part in parts]
    hbm = pl.BlockSpec(memory_space=pltpu.HBM)
    return pl.pallas_call(
        settle_kernel,
        out_shape=tuple(jax.ShapeDtypeStruct(part.shape, part.dtype) for part in others),
        in_specs=[hbm] * 3,
        out_specs=(hbm,) * 3,
        input_output_aliases={0: 0, 1: 1, 2: 2},
        cost_estimate=pl.CostEstimate(
            flops=10**11, transcendentals=0, bytes_accessed=4 * 10**8),
        name="settle",
    )(*others)


def expert_kernel(came_ref, gate_ref, up_ref, down_ref, gate_other_ref, up_other_ref,
                  down_other_ref, out_ref, held_ref, both_ref, down_all_ref,
                  wide_ref, rows_ref, hidden_ref, result_ref, came_sem, both_sem, down_sem):
    count, parts = came_ref.shape[0], came_ref.shape[1]
    half_ff, width = gate_ref.shape
    columns = down_ref.shape[1]
    pitch = padded(parts)
    mine = lax.axis_index("fsdp")

    def fetch(b):
        at = pl.multiple_of(b * ROW_BLOCK, ROW_BLOCK)
        return pltpu.make_async_copy(came_ref.at[pl.ds(at, ROW_BLOCK)],
                                     held_ref.at[pl.ds(at, ROW_BLOCK)], came_sem.at[b])

    @pl.loop(0, count // ROW_BLOCK)
    def _(b):
        fetch(b).start()

    pairs = ((gate_ref, gate_other_ref), (up_ref, up_other_ref))
    pieces = []
    for low in range(0, 2 * half_ff, PIECE):
        at, own = low % half_ff, low < half_ff
        step, inside = low // FF_BLOCK, low % FF_BLOCK
        for which, (first, second) in enumerate(pairs):
            to = (2 * step + which) * FF_BLOCK + inside
            pieces.append(pltpu.make_async_copy(
                (first if own else second).at[at:at + PIECE],
                both_ref.at[to:to + PIECE], both_sem.at[len(pieces)]))
    per_step = len(pairs) * FF_BLOCK // PIECE
    down_copies = []
    for which, (part, index) in enumerate(((down_ref, mine), (down_other_ref, 1 - mine))):
        to = pl.multiple_of(index * columns, columns)
        for half, owner in enumerate((mine, 1 - mine)):
            at = pl.multiple_of(owner * half_ff, half_ff)
            down_copies.append(pltpu.make_async_copy(
                part.at[pl.ds(at, half_ff)],
                down_all_ref.at[half * half_ff:(half + 1) * half_ff, pl.ds(to, columns)],
                down_sem.at[2 * which + half]))

    def relay(b):
        fetch(b).wait()
        at = pl.multiple_of(b * ROW_BLOCK, ROW_BLOCK)
        for row in range(ROW_BLOCK):
            wide_ref[row * pitch:row * pitch + parts, :] = held_ref[at + row].astype(jnp.float32)
        for part in range(parts):
            rows_ref[pl.ds(at, ROW_BLOCK), part * LANES:(part + 1) * LANES] = (
                wide_ref[pl.ds(part, ROW_BLOCK, stride=pitch), :].astype(rows_ref.dtype))

    blocks = count // ROW_BLOCK
    steps = 2 * half_ff // FF_BLOCK
    for step in range(steps):
        for copy in pieces[step * per_step:(step + 1) * per_step]:
            copy.start()
        pl.loop(step * blocks // steps, (step + 1) * blocks // steps)(relay)
    for copy in down_copies:
        copy.start()

    contract = (((1,), (1,)), ((), ()))
    for step in range(steps):
        for copy in pieces[step * per_step:(step + 1) * per_step]:
            copy.wait()
        low = step * FF_BLOCK
        both = lax.dot_general(rows_ref[...], both_ref[2 * low:2 * (low + FF_BLOCK)], contract,
                               preferred_element_type=jnp.float32)
        gate, up = both[:, :FF_BLOCK], both[:, FF_BLOCK:]
        hidden = gate / (1.0 + jnp.exp(-gate)) * up
        hidden_ref[:, low:low + FF_BLOCK] = hidden.astype(hidden_ref.dtype)
    for copy in down_copies:
        copy.wait()

    out_parts = COLUMN_BLOCK // LANES
    out_pitch = padded(out_parts)
    products = COLUMN_BLOCK // PRODUCT
    column_blocks = width // COLUMN_BLOCK

    def convert(block, at, rows):
        for row in range(rows):
            first = (at + row) * out_pitch
            if not isinstance(first, int):
                first = pl.multiple_of(first, 8)
            out_ref[at + row, block * out_parts:(block + 1) * out_parts] = (
                result_ref[block % 2, pl.ds(first, out_parts), :].astype(out_ref.dtype))

    for block in range(column_blocks):
        for piece in range(products):
            low = block * COLUMN_BLOCK + piece * PRODUCT
            result = jnp.dot(hidden_ref[...], down_all_ref[:, low:low + PRODUCT],
                             preferred_element_type=jnp.float32)
            for part in range(PRODUCT // LANES):
                at = piece * (PRODUCT // LANES) + part
                result_ref[block % 2, pl.ds(at, count, stride=out_pitch), :] = (
                    result[:, part * LANES:(part + 1) * LANES])
            if block > 0:
                convert(block - 1, piece * (count // products), count // products)

    @pl.loop(0, count // ROW_BLOCK)
    def _(b):
        convert(column_blocks - 1, b * ROW_BLOCK, ROW_BLOCK)


def expert(came, own, other):
    count, parts, _ = came.shape
    half_ff, width = own[0].shape
    ff, dtype = 2 * half_ff, came.dtype
    steps = ff // PIECE
    anywhere = pl.BlockSpec(memory_space=pl.ANY)
    return pl.pallas_call(
        expert_kernel,
        out_shape=jax.ShapeDtypeStruct(came.shape, dtype),
        in_specs=[anywhere] * 7,
        out_specs=pl.BlockSpec(memory_space=pltpu.VMEM),
        scratch_shapes=[
            pltpu.VMEM(came.shape, dtype),
            pltpu.VMEM((2 * ff, width), dtype),
            pltpu.VMEM((ff, width), dtype),
            pltpu.VMEM((ROW_BLOCK * padded(parts), LANES), jnp.float32),
            pltpu.VMEM((count, width), dtype),
            pltpu.VMEM((count, ff), dtype),
            pltpu.VMEM((2, count * padded(COLUMN_BLOCK // LANES), LANES), jnp.float32),
            pltpu.SemaphoreType.DMA((count // ROW_BLOCK,)),
            pltpu.SemaphoreType.DMA((2 * steps,)),
            pltpu.SemaphoreType.DMA((4,)),
        ],
        compiler_params=pltpu.CompilerParams(vmem_limit_bytes=EXPERT_LIMIT),
        cost_estimate=pl.CostEstimate(
            flops=6 * count * ff * width, transcendentals=count * ff,
            bytes_accessed=2 * (3 * ff * width + 2 * count * width)),
        name="expert",
    )(came, *own, *other)


def combine_kernel(place_ref, share_ref, back_ref, out_ref, total_ref):
    top_count, tok_count = share_ref.shape
    parts = back_ref.shape[1]
    pitch = padded(parts)

    @pl.loop(0, tok_count, unroll=4)
    def _(t):
        terms = [share_ref[k, t] * back_ref[place_ref[k, t]].astype(jnp.float32)
                 for k in range(top_count)]
        while len(terms) > 1:
            terms = [left + right for left, right in zip(terms[::2], terms[1::2])]
        total = terms[0]
        total_ref[pl.ds(pl.multiple_of(t * pitch, 8), parts), :] = total

    for part in range(parts):
        out_ref[:, part * LANES:(part + 1) * LANES] = (
            total_ref[pl.ds(part, tok_count, stride=pitch), :].astype(out_ref.dtype))


def combine(place, share, back):
    tok_count = share.shape[1]
    parts = back.shape[1]
    smem = pl.BlockSpec(memory_space=pltpu.SMEM)
    vmem = pl.BlockSpec(memory_space=pltpu.VMEM)
    return pl.pallas_call(
        combine_kernel,
        out_shape=jax.ShapeDtypeStruct((tok_count, parts * LANES), back.dtype),
        in_specs=[smem, smem, vmem],
        out_specs=vmem,
        scratch_shapes=[pltpu.VMEM((tok_count * padded(parts), LANES), jnp.float32)],
        compiler_params=pltpu.CompilerParams(vmem_limit_bytes=SMALL_LIMIT),
        name="combine",
    )(place, share, back)


def exchange(rows, experts_count):
    sent = rows.reshape(experts_count, -1, LANES)
    came = lax.all_to_all(sent, "expert", split_axis=0, concat_axis=0, tiled=True)
    return came.reshape(rows.shape)


def body(tokens, expert_ids, route_weight, gate_weight, up_weight, down_weight):
    experts_count = lax.axis_size("expert") * gate_weight.shape[0]
    tok_count, top_count = expert_ids.shape
    capacity = tok_count * top_count // experts_count + 1
    late = (lax.axis_index("fsdp") * STAGGER).astype(jnp.int32).reshape(1)
    sent, place = dispatch(late, expert_ids.T, tokens, experts_count, capacity)
    came = exchange(sent, experts_count)
    own = (gate_weight[0], up_weight[0], down_weight[0])
    back = exchange(expert(came, own, partner_weights(own)), experts_count)
    return combine(place, route_weight.T, back)


def solution(mesh):
    placed = (
        P(("fsdp", "expert"), None),
        P(("fsdp", "expert"), None),
        P(("fsdp", "expert"), None),
        P("expert", "fsdp", None),
        P("expert", "fsdp", None),
        P("expert", None, "fsdp"),
    )
    return jax.shard_map(
        body, mesh=mesh, in_specs=placed, out_specs=P(("fsdp", "expert"), None), check_vma=False
    )
```

```python
import functools

import jax
import jax.numpy as jnp
from jax import lax
from jax.experimental import pallas as pl
from jax.experimental.pallas import tpu as pltpu
from jax.sharding import PartitionSpec as P

LANES = 128
ROW_BLOCK = 64
FF_BLOCK = 256
PIECE = 128
PRODUCT = 512
COLUMN_BLOCK = 2048
STAGGER = 654
EXPERT_GROUP = 4
DISPATCH_LIMIT = 60 * 1024 * 1024
SMALL_LIMIT = 14 * 1024 * 1024
EXPERT_LIMIT = 50 * 1024 * 1024


def padded(parts):
    return parts + 8


def dispatch_kernel(capacity, late_ref, ids_ref, tokens_ref, out_ref, place_ref,
                    wide_ref, rows_ref, stage_ref, table_ref, where_ref, table_sem, out_sem):
    top_count, tok_count = ids_ref.shape
    parts = rows_ref.shape[1]
    experts_count = out_ref.shape[0] // capacity
    pitch = padded(parts)
    ids = ids_ref[...]
    name = lax.broadcasted_iota(jnp.int32, (experts_count, tok_count), 0)
    token = lax.broadcasted_iota(jnp.int32, (experts_count, tok_count), 1)
    chosen = jnp.zeros((experts_count, tok_count), jnp.float32)
    for k in range(top_count):
        chosen += (ids[k:k + 1] == name).astype(jnp.float32)
    earlier = (lax.broadcasted_iota(jnp.int32, (tok_count, tok_count), 0)
               < lax.broadcasted_iota(jnp.int32, (tok_count, tok_count), 1))
    rank = jnp.dot(chosen.astype(jnp.bfloat16),
                   earlier.astype(jnp.float32).astype(jnp.bfloat16),
                   preferred_element_type=jnp.float32)
    held = jnp.where(chosen > 0.0, rank, -1.0)
    lane = lax.broadcasted_iota(jnp.int32, (experts_count, LANES), 1)
    table = jnp.zeros((experts_count, LANES), jnp.float32)
    for slot in range(capacity):
        source = jnp.sum(jnp.where(held == float(slot), token.astype(jnp.float32), 0.0),
                         axis=1, keepdims=True)
        table = jnp.where(lane == slot, source, table)
    table_ref[...] = table.astype(jnp.int32)
    copy = pltpu.make_async_copy(table_ref, where_ref, table_sem)
    copy.start()
    waited = lax.fori_loop(
        0, late_ref[0], lambda i, a: jnp.sin(a) * 0.5 + 1.0,
        jnp.ones(place_ref.shape, jnp.float32)).astype(jnp.int32)
    place_ref[...] = waited
    for part in range(parts):
        wide_ref[pl.ds(part, tok_count, stride=pitch), :] = (
            tokens_ref[:, part * LANES:(part + 1) * LANES].astype(jnp.float32))
    for t in range(tok_count):
        rows_ref[t] = wide_ref[t * pitch:t * pitch + parts, :].astype(rows_ref.dtype)
    copy.wait()

    group = EXPERT_GROUP * capacity

    def send(g):
        at = pl.multiple_of(g * group, group)
        return pltpu.make_async_copy(stage_ref.at[pl.ds(at, group)],
                                     out_ref.at[pl.ds(at, group)], out_sem.at[g])

    @pl.loop(0, experts_count // EXPERT_GROUP)
    def _(g):
        @pl.loop(0, EXPERT_GROUP, unroll=4)
        def _(i):
            e = g * EXPERT_GROUP + i
            for slot in range(capacity):
                stage_ref[e * capacity + slot] = rows_ref[where_ref[e, slot]]
        send(g).start()

    start = rank + (name * capacity).astype(jnp.float32)
    for k in range(top_count):
        place = jnp.sum(jnp.where(ids[k:k + 1] == name, start, 0.0), axis=0, keepdims=True)
        place_ref[k:k + 1, :tok_count] = place.astype(jnp.int32)

    @pl.loop(0, experts_count // EXPERT_GROUP)
    def _(g):
        send(g).wait()


def dispatch(late, ids, tokens, experts_count, capacity):
    top_count, tok_count = ids.shape
    parts = tokens.shape[1] // LANES
    count = experts_count * capacity
    vmem = pl.BlockSpec(memory_space=pltpu.VMEM)
    smem = pl.BlockSpec(memory_space=pltpu.SMEM)
    return pl.pallas_call(
        functools.partial(dispatch_kernel, capacity),
        out_shape=(
            jax.ShapeDtypeStruct((count, parts, LANES), tokens.dtype),
            jax.ShapeDtypeStruct((top_count, LANES), jnp.int32),
        ),
        in_specs=[smem, vmem, vmem],
        out_specs=(pl.BlockSpec(memory_space=pltpu.HBM), vmem),
        scratch_shapes=[
            pltpu.VMEM((tok_count * padded(parts), LANES), jnp.float32),
            pltpu.VMEM((tok_count, parts, LANES), tokens.dtype),
            pltpu.VMEM((count, parts, LANES), tokens.dtype),
            pltpu.VMEM((experts_count, LANES), jnp.int32),
            pltpu.SMEM((experts_count, LANES), jnp.int32),
            pltpu.SemaphoreType.DMA,
            pltpu.SemaphoreType.DMA((experts_count // EXPERT_GROUP,)),
        ],
        compiler_params=pltpu.CompilerParams(vmem_limit_bytes=DISPATCH_LIMIT),
        name="dispatch",
    )(late, ids, tokens)


def settle_kernel(gate_ref, up_ref, down_ref, gate_out_ref, up_out_ref, down_out_ref):
    del gate_ref, up_ref, down_ref, gate_out_ref, up_out_ref, down_out_ref


def partner_weights(parts):
    others = [lax.ppermute(part, "fsdp", [(0, 1), (1, 0)]) for part in parts]
    hbm = pl.BlockSpec(memory_space=pltpu.HBM)
    return pl.pallas_call(
        settle_kernel,
        out_shape=tuple(jax.ShapeDtypeStruct(part.shape, part.dtype) for part in others),
        in_specs=[hbm] * 3,
        out_specs=(hbm,) * 3,
        input_output_aliases={0: 0, 1: 1, 2: 2},
        cost_estimate=pl.CostEstimate(
            flops=10**11, transcendentals=0, bytes_accessed=4 * 10**8),
        name="settle",
    )(*others)


def expert_kernel(came_ref, gate_ref, up_ref, down_ref, gate_other_ref, up_other_ref,
                  down_other_ref, out_ref, held_ref, both_ref, down_all_ref,
                  wide_ref, rows_ref, hidden_ref, result_ref, came_sem, both_sem, down_sem):
    count, parts = came_ref.shape[0], came_ref.shape[1]
    half_ff, width = gate_ref.shape
    columns = down_ref.shape[1]
    pitch = padded(parts)
    mine = lax.axis_index("fsdp")

    def fetch(b):
        at = pl.multiple_of(b * ROW_BLOCK, ROW_BLOCK)
        return pltpu.make_async_copy(came_ref.at[pl.ds(at, ROW_BLOCK)],
                                     held_ref.at[pl.ds(at, ROW_BLOCK)], came_sem.at[b])

    @pl.loop(0, count // ROW_BLOCK)
    def _(b):
        fetch(b).start()

    pairs = ((gate_ref, gate_other_ref), (up_ref, up_other_ref))
    pieces = []
    for low in range(0, 2 * half_ff, PIECE):
        at, own = low % half_ff, low < half_ff
        step, inside = low // FF_BLOCK, low % FF_BLOCK
        for which, (first, second) in enumerate(pairs):
            to = (2 * step + which) * FF_BLOCK + inside
            pieces.append(pltpu.make_async_copy(
                (first if own else second).at[at:at + PIECE],
                both_ref.at[to:to + PIECE], both_sem.at[len(pieces)]))
    per_step = len(pairs) * FF_BLOCK // PIECE
    down_copies = []
    for which, (part, index) in enumerate(((down_ref, mine), (down_other_ref, 1 - mine))):
        to = pl.multiple_of(index * columns, columns)
        for half, owner in enumerate((mine, 1 - mine)):
            at = pl.multiple_of(owner * half_ff, half_ff)
            down_copies.append(pltpu.make_async_copy(
                part.at[pl.ds(at, half_ff)],
                down_all_ref.at[half * half_ff:(half + 1) * half_ff, pl.ds(to, columns)],
                down_sem.at[2 * which + half]))

    def relay(b):
        fetch(b).wait()
        at = pl.multiple_of(b * ROW_BLOCK, ROW_BLOCK)
        for row in range(ROW_BLOCK):
            wide_ref[row * pitch:row * pitch + parts, :] = held_ref[at + row].astype(jnp.float32)
        for part in range(parts):
            rows_ref[pl.ds(at, ROW_BLOCK), part * LANES:(part + 1) * LANES] = (
                wide_ref[pl.ds(part, ROW_BLOCK, stride=pitch), :].astype(rows_ref.dtype))

    blocks = count // ROW_BLOCK
    steps = 2 * half_ff // FF_BLOCK
    for step in range(steps):
        for copy in pieces[step * per_step:(step + 1) * per_step]:
            copy.start()
        pl.loop(step * blocks // steps, (step + 1) * blocks // steps)(relay)
    for copy in down_copies:
        copy.start()

    contract = (((1,), (1,)), ((), ()))
    for step in range(steps):
        for copy in pieces[step * per_step:(step + 1) * per_step]:
            copy.wait()
        low = step * FF_BLOCK
        both = lax.dot_general(rows_ref[...], both_ref[2 * low:2 * (low + FF_BLOCK)], contract,
                               preferred_element_type=jnp.float32)
        gate, up = both[:, :FF_BLOCK], both[:, FF_BLOCK:]
        hidden = gate / (1.0 + jnp.exp(-gate)) * up
        hidden_ref[:, low:low + FF_BLOCK] = hidden.astype(hidden_ref.dtype)
    for copy in down_copies:
        copy.wait()

    out_parts = COLUMN_BLOCK // LANES
    out_pitch = padded(out_parts)
    products = COLUMN_BLOCK // PRODUCT
    column_blocks = width // COLUMN_BLOCK

    def convert(block, at, rows):
        for row in range(rows):
            first = (at + row) * out_pitch
            if not isinstance(first, int):
                first = pl.multiple_of(first, 8)
            out_ref[at + row, block * out_parts:(block + 1) * out_parts] = (
                result_ref[block % 2, pl.ds(first, out_parts), :].astype(out_ref.dtype))

    for block in range(column_blocks):
        for piece in range(products):
            low = block * COLUMN_BLOCK + piece * PRODUCT
            result = jnp.dot(hidden_ref[...], down_all_ref[:, low:low + PRODUCT],
                             preferred_element_type=jnp.float32)
            for part in range(PRODUCT // LANES):
                at = piece * (PRODUCT // LANES) + part
                result_ref[block % 2, pl.ds(at, count, stride=out_pitch), :] = (
                    result[:, part * LANES:(part + 1) * LANES])
            if block > 0:
                convert(block - 1, piece * (count // products), count // products)

    @pl.loop(0, count // ROW_BLOCK)
    def _(b):
        convert(column_blocks - 1, b * ROW_BLOCK, ROW_BLOCK)


def expert(came, own, other):
    count, parts, _ = came.shape
    half_ff, width = own[0].shape
    ff, dtype = 2 * half_ff, came.dtype
    steps = ff // PIECE
    anywhere = pl.BlockSpec(memory_space=pl.ANY)
    return pl.pallas_call(
        expert_kernel,
        out_shape=jax.ShapeDtypeStruct(came.shape, dtype),
        in_specs=[anywhere] * 7,
        out_specs=pl.BlockSpec(memory_space=pltpu.VMEM),
        scratch_shapes=[
            pltpu.VMEM(came.shape, dtype),
            pltpu.VMEM((2 * ff, width), dtype),
            pltpu.VMEM((ff, width), dtype),
            pltpu.VMEM((ROW_BLOCK * padded(parts), LANES), jnp.float32),
            pltpu.VMEM((count, width), dtype),
            pltpu.VMEM((count, ff), dtype),
            pltpu.VMEM((2, count * padded(COLUMN_BLOCK // LANES), LANES), jnp.float32),
            pltpu.SemaphoreType.DMA((count // ROW_BLOCK,)),
            pltpu.SemaphoreType.DMA((2 * steps,)),
            pltpu.SemaphoreType.DMA((4,)),
        ],
        compiler_params=pltpu.CompilerParams(vmem_limit_bytes=EXPERT_LIMIT),
        cost_estimate=pl.CostEstimate(
            flops=6 * count * ff * width, transcendentals=count * ff,
            bytes_accessed=2 * (3 * ff * width + 2 * count * width)),
        name="expert",
    )(came, *own, *other)


def combine_kernel(place_ref, share_ref, back_ref, out_ref, total_ref):
    top_count, tok_count = share_ref.shape
    parts = back_ref.shape[1]
    pitch = padded(parts)

    @pl.loop(0, tok_count, unroll=4)
    def _(t):
        terms = [share_ref[k, t] * back_ref[place_ref[k, t]].astype(jnp.float32)
                 for k in range(top_count)]
        while len(terms) > 1:
            terms = [left + right for left, right in zip(terms[::2], terms[1::2])]
        total = terms[0]
        total_ref[pl.ds(pl.multiple_of(t * pitch, 8), parts), :] = total

    for part in range(parts):
        out_ref[:, part * LANES:(part + 1) * LANES] = (
            total_ref[pl.ds(part, tok_count, stride=pitch), :].astype(out_ref.dtype))


def combine(place, share, back):
    tok_count = share.shape[1]
    parts = back.shape[1]
    smem = pl.BlockSpec(memory_space=pltpu.SMEM)
    vmem = pl.BlockSpec(memory_space=pltpu.VMEM)
    return pl.pallas_call(
        combine_kernel,
        out_shape=jax.ShapeDtypeStruct((tok_count, parts * LANES), back.dtype),
        in_specs=[smem, smem, vmem],
        out_specs=vmem,
        scratch_shapes=[pltpu.VMEM((tok_count * padded(parts), LANES), jnp.float32)],
        compiler_params=pltpu.CompilerParams(vmem_limit_bytes=SMALL_LIMIT),
        name="combine",
    )(place, share, back)


def exchange(rows, experts_count):
    sent = rows.reshape(experts_count, -1, LANES)
    came = lax.all_to_all(sent, "expert", split_axis=0, concat_axis=0, tiled=True)
    return came.reshape(rows.shape)


def body(tokens, expert_ids, route_weight, gate_weight, up_weight, down_weight):
    experts_count = lax.axis_size("expert") * gate_weight.shape[0]
    tok_count, top_count = expert_ids.shape
    capacity = tok_count * top_count // experts_count + 1
    late = ((1 - lax.axis_index("fsdp")) * STAGGER).astype(jnp.int32).reshape(1)
    sent, place = dispatch(late, expert_ids.T, tokens, experts_count, capacity)
    came = exchange(sent, experts_count)
    own = (gate_weight[0], up_weight[0], down_weight[0])
    back = exchange(expert(came, own, partner_weights(own)), experts_count)
    return combine(place, route_weight.T, back)


def solution(mesh):
    placed = (
        P(("fsdp", "expert"), None),
        P(("fsdp", "expert"), None),
        P(("fsdp", "expert"), None),
        P("expert", "fsdp", None),
        P("expert", "fsdp", None),
        P("expert", None, "fsdp"),
    )
    return jax.shard_map(
        body, mesh=mesh, in_specs=placed, out_specs=P(("fsdp", "expert"), None), check_vma=False
    )
```
